32 devices in a mesh: query: 8 (over z, y), item: 4 (over x, core).
Axes of the slice: x: 2, y: 2, z: 4, core: 2. Of those that a mesh axis runs over, the one named last changes fastest.
Arguments:
- query_emb: bfloat16 [2048, 256], P(('query', 'item')), may hold values from -400 to 400
- targets: int32 [2048], P('query'), may hold values from 0 to 8191, as said below
- eligible_tiles: int32 [32, 32], P('query', 'item'), may hold values from 0 to 1, as said below
- item_feats: bfloat16 [4, 2048, 512], P('item', 'query'), may hold values from -6 to 6
- w_first: bfloat16 [512, 1024], replicated, may hold values from -0.25 to 0.25
- w_second: bfloat16 [1024, 256], replicated, may hold values from -0.1875 to 0.1875
Outputs:
- loss: float32 [2048], P(('query', 'item'))
- query_grad: float32 [2048, 256], P(('query', 'item'))
- w_first_grad: float32 [512, 1024], replicated
- w_second_grad: float32 [1024, 256], replicated
The draws below stay inside these ranges and needn't reach their ends.
Inputs may be any that keep to these rules, and one draw needn't show every extreme that they name: `eligible_tiles`: every row has at least one 1. The block targets[q] // 256 is marked 1 in row q // 64 of eligible_tiles.
All inputs are finite; a program needn't handle non-finite values.
Results may differ from the reference program's by a relative error of at most 0.007.
Values may be sent and summed in bfloat16 or wider, within the bound.
A program may use at most 64 MiB of HBM per device.

```python
import math
import jax
import jax.numpy as jnp
from jax import lax

DIN = 512
HID = 1024
E = 256
Q_DEV = 64
I_DEV = 256
NQ = 2048
ITEMS = 8192
QBLOCKS = 32
IBLOCKS = 32
TILE = 2048
N_ITEM = 4


def eligibility(key):
    key_row, key_col, key_roll, key_force = jax.random.split(jax.random.fold_in(key, 11), 4)
    row_pct = jax.random.randint(key_row, (QBLOCKS, 1), 8, 53)
    col_pct = jax.random.randint(key_col, (1, IBLOCKS), 50, 151)
    rolled = jax.random.randint(key_roll, (QBLOCKS, IBLOCKS), 0, 10000)
    live_set = rolled < row_pct * col_pct
    forced = jax.random.randint(key_force, (QBLOCKS,), 0, IBLOCKS)
    blocks = jnp.arange(IBLOCKS, dtype=jnp.int32)
    live_set = live_set | (blocks[None, :] == forced[:, None])
    return live_set.astype(jnp.int32)


def draw_eligible_tiles(key, part):
    return eligibility(key)


def draw_targets(key, part):
    tiles = eligibility(key)
    key_pick, key_row = jax.random.split(jax.random.fold_in(key, 23))
    per_query = jnp.repeat(tiles, Q_DEV, axis=0)
    blocks = jnp.arange(IBLOCKS, dtype=jnp.int32)
    ranked = jax.random.randint(key_pick, (NQ, IBLOCKS), 0, 1 << 20) * IBLOCKS + blocks[None, :]
    ranked = jnp.where(per_query > 0, ranked, -1)
    chosen = jnp.argmax(ranked, axis=1).astype(jnp.int32)
    offsets = jax.random.randint(key_row, (NQ,), 0, I_DEV)
    return chosen * I_DEV + offsets


def draw_query_emb(key, part):
    key_base = jax.random.fold_in(jax.random.fold_in(key, 37), 0)
    key_shared = jax.random.fold_in(jax.random.fold_in(key, 37), 3)
    values = jax.random.truncated_normal(key_base, -4.0, 4.0, (NQ, E), jnp.float32)
    shared = jax.random.truncated_normal(key_shared, -3.0, 3.0, (1, E), jnp.float32)
    values = values + shared
    return values.astype(jnp.bfloat16)


def block_scale(stream_key, extent, pieces, least, high):
    factor_of = 1.0
    for dim, blocks in pieces:
        draws = jax.random.uniform(jax.random.fold_in(jax.random.fold_in(stream_key, 6), dim), (blocks,), jnp.float32, least / len(pieces), high / len(pieces))
        factor_of = factor_of * jnp.repeat(jnp.exp(draws), extent[dim] // blocks).reshape((-1,) + (1,) * (len(extent) - 1 - dim))
    return factor_of


def normal_values(key, shape, spread, limit, pieces=(), kind=jnp.bfloat16):
    array = jax.random.normal(key, shape, jnp.float32) * spread
    if len(pieces) > 0:
        array = block_scale(key, shape, pieces, -0.22, 0.18) * array
    return jnp.clip(array, min=-limit, max=limit).astype(kind)


def setup_inputs(seed: int = 0) -> dict:
    splits = jax.random.split(jax.random.key(seed), 7)
    query_emb = draw_query_emb(jax.random.fold_in(splits[6], 71), 0)
    targets = draw_targets(jax.random.fold_in(splits[6], 71), 0)
    eligible_tiles = draw_eligible_tiles(jax.random.fold_in(splits[6], 71), 0)
    item_feats = normal_values(splits[3], (N_ITEM, TILE, DIN), 1.0, 6.0, ((0, 4), (1, 8)))
    w_first = normal_values(splits[4], (DIN, HID), DIN ** -0.5, 0.25)
    w_second = normal_values(splits[5], (HID, E), HID ** -0.5, 0.1875)
    return {"query_emb": query_emb, "targets": targets, "eligible_tiles": eligible_tiles, "item_feats": item_feats, "w_first": w_first, "w_second": w_second}


def reference(query_emb, targets, eligible_tiles, item_feats, w_first, w_second):
    tokens = item_feats.reshape(ITEMS, DIN)
    tok_wide = tokens.astype(jnp.float32)
    pre_act = jnp.dot(tok_wide, w_first.astype(jnp.float32), preferred_element_type=jnp.float32)
    hidden = lax.optimization_barrier(jax.nn.silu(pre_act).astype(jnp.bfloat16)).astype(jnp.float32)
    item_emb = jnp.dot(hidden, w_second.astype(jnp.float32), preferred_element_type=jnp.float32)
    emb_wide = lax.optimization_barrier(item_emb.astype(jnp.bfloat16)).astype(jnp.float32)
    columns = jnp.arange(ITEMS, dtype=jnp.int32)

    def one_block(emb_grad, block_idx):
        queries = lax.dynamic_slice_in_dim(query_emb, block_idx * Q_DEV, Q_DEV, 0).astype(jnp.float32)
        wanted = lax.dynamic_slice_in_dim(targets, block_idx * Q_DEV, Q_DEV, 0)
        live_cols = jnp.repeat(eligible_tiles[block_idx] > 0, I_DEV)[None, :]
        scores = 0.25 * jnp.dot(queries, emb_wide.T, preferred_element_type=jnp.float32)
        masked = jnp.where(live_cols, scores, -1e+30)
        run_max = lax.optimization_barrier(jnp.max(masked, axis=1))
        run_sum = lax.optimization_barrier(jnp.sum(jnp.where(live_cols, jnp.exp(masked - run_max[:, None]), 0.0), axis=1))
        log_norm = run_max + jnp.log(run_sum)
        is_target = columns[None, :] == wanted[:, None]
        positive = lax.optimization_barrier(jnp.sum(jnp.where(is_target, scores, 0.0), axis=1))
        softmax_w = jnp.where(live_cols, jnp.exp(masked - log_norm[:, None]), 0.0)
        coeffs = softmax_w - is_target.astype(jnp.float32)
        coeffs = lax.optimization_barrier(coeffs.astype(jnp.bfloat16)).astype(jnp.float32)
        q_grads = 0.25 * jnp.dot(coeffs, emb_wide, preferred_element_type=jnp.float32)
        emb_grad = emb_grad + 0.25 * jnp.dot(coeffs.T, queries, preferred_element_type=jnp.float32)
        return (emb_grad, (log_norm - positive, q_grads))
    start_grad = jnp.zeros((ITEMS, E), jnp.float32)
    emb_grad, outputs = lax.scan(one_block, start_grad, jnp.arange(QBLOCKS, dtype=jnp.int32))
    loss = outputs[0].reshape(NQ)
    query_grad = outputs[1].reshape(NQ, E)
    grad_b = lax.optimization_barrier(emb_grad.astype(jnp.bfloat16)).astype(jnp.float32)
    grad_scale = 1.0 / math.sqrt(ITEMS)
    w_second_grad = jnp.dot(hidden.T, grad_b, preferred_element_type=jnp.float32) * grad_scale
    hid_grad = jnp.dot(grad_b, w_second.astype(jnp.float32).T, preferred_element_type=jnp.float32)
    gate_sig = jax.nn.sigmoid(pre_act)
    pre_grad = hid_grad * gate_sig * (1.0 + pre_act * (1.0 - gate_sig))
    pre_grad = lax.optimization_barrier(pre_grad.astype(jnp.bfloat16)).astype(jnp.float32)
    w_first_grad = jnp.dot(tok_wide.T, pre_grad, preferred_element_type=jnp.float32) * grad_scale
    return (loss, query_grad, w_first_grad, w_second_grad)
```

```python
import math

import jax
import jax.numpy as jnp
from jax import lax
from jax.sharding import PartitionSpec as P

BOTH = ("query", "item")


def on_device(query_emb, targets, eligible_tiles, item_feats, w_first, w_second):
    q_rows = query_emb.shape[0]
    item_count = lax.axis_size("item")
    query_count = lax.axis_size("query")
    item_pos = lax.axis_index("item")
    query_pos = lax.axis_index("query")
    tokens = item_feats.reshape(item_feats.shape[1], item_feats.shape[2])
    block_rows = tokens.shape[0]
    queries = lax.all_gather(query_emb, "query", axis=0, tiled=True)
    own_targets = lax.dynamic_slice_in_dim(targets, item_pos * q_rows, q_rows, 0)
    small = jnp.concatenate([eligible_tiles.reshape(-1), own_targets])
    small = lax.all_gather(small, BOTH, axis=0).reshape(query_count, item_count, -1)
    flags = small[:, :, : eligible_tiles.size].reshape((query_count, item_count) + eligible_tiles.shape)
    flags = lax.dynamic_slice(
        flags, (0, 0, item_pos, query_pos), (query_count, item_count, 1, 1)
    ).reshape(query_count, item_count)
    wanted = lax.dynamic_slice_in_dim(small[:, :, eligible_tiles.size :], item_pos, 1, 1).reshape(-1)

    pre_act = jnp.dot(tokens, w_first, preferred_element_type=jnp.float32)
    hidden = jax.nn.silu(pre_act).astype(jnp.bfloat16)
    own_emb = jnp.dot(hidden, w_second, preferred_element_type=jnp.float32).astype(jnp.bfloat16)
    items = lax.all_gather(own_emb, "item", axis=0, tiled=True)
    block_of = jnp.arange(item_count, dtype=jnp.int32) * query_count + query_pos
    item_ids = (
        block_of[:, None] * block_rows + jnp.arange(block_rows, dtype=jnp.int32)[None, :]
    ).reshape(-1)
    live = jnp.broadcast_to(
        flags[:, None, :, None] > 0, (query_count, q_rows, item_count, block_rows)
    ).reshape(query_count * q_rows, item_count * block_rows)
    scores = 0.25 * jnp.einsum("qe,ie->qi", queries, items, preferred_element_type=jnp.float32)
    hit = item_ids[None, :] == wanted[:, None]
    masked = jnp.where(live, scores, -1e30)
    top = jnp.max(masked, axis=1)
    total = jnp.sum(jnp.where(live, jnp.exp(masked - top[:, None]), 0.0), axis=1)
    positive = jnp.sum(jnp.where(hit, scores, 0.0), axis=1)
    stats = lax.all_gather(jnp.stack([top, total, positive]), "query", axis=0)
    all_top = jnp.max(stats[:, 0], axis=0)
    all_total = jnp.sum(stats[:, 1] * jnp.exp(stats[:, 0] - all_top[None]), axis=0)
    log_norm = all_top + jnp.log(all_total)
    loss = lax.dynamic_slice_in_dim(
        log_norm - jnp.sum(stats[:, 2], axis=0), query_pos * q_rows, q_rows, 0
    )
    weights = jnp.where(live, jnp.exp(masked - log_norm[:, None]), 0.0)
    coeffs = (weights - hit.astype(jnp.float32)).astype(jnp.bfloat16)
    e_part = 0.25 * jnp.einsum("qi,qe->ie", coeffs, queries, preferred_element_type=jnp.float32)
    own_grad = lax.psum_scatter(e_part, "item", scatter_dimension=0, tiled=True).astype(
        jnp.bfloat16
    )
    q_part = 0.25 * jnp.dot(coeffs, items, preferred_element_type=jnp.float32)
    query_grad = lax.psum_scatter(q_part, "query", scatter_dimension=0, tiled=True)
    second_term = jnp.einsum("ih,ie->he", hidden, own_grad, preferred_element_type=jnp.float32)
    hid_grad = jnp.einsum("ie,he->ih", own_grad, w_second, preferred_element_type=jnp.float32)
    gate_sig = jax.nn.sigmoid(pre_act)
    pre_grad = (hid_grad * gate_sig * (1.0 + pre_act * (1.0 - gate_sig))).astype(jnp.bfloat16)
    first_term = jnp.einsum("id,ih->dh", tokens, pre_grad, preferred_element_type=jnp.float32)
    tower_sums = lax.psum((first_term, second_term), BOTH)
    grad_scale = 1.0 / math.sqrt(block_rows * query_count * item_count)
    return (loss, query_grad, tower_sums[0] * grad_scale, tower_sums[1] * grad_scale)


def solution(mesh):
    return jax.shard_map(
        on_device,
        mesh=mesh,
        in_specs=(
            P(("query", "item"), None),
            P("query"),
            P("query", "item"),
            P("item", "query", None),
            P(),
            P(),
        ),
        out_specs=(P(("query", "item")), P(("query", "item"), None), P(), P()),
        check_vma=False,
    )
```

```python
import functools
import math

import jax
import jax.numpy as jnp
from jax import lax
from jax.experimental import pallas as pl
from jax.experimental.pallas import tpu as pltpu
from jax.sharding import PartitionSpec as P

F32 = jnp.float32
BF16 = jnp.bfloat16


def dot(a, b, contract):
    return lax.dot_general(a, b, ((contract[:1], contract[1:]), ((), ())), preferred_element_type=F32)


def rows(start, size):
    return pl.ds(pl.multiple_of(start, math.gcd(size, 256)), size)


def window_kernel(
    shape,
    query_ref, meta_ref, tokens_ref, w1_ref, w2_ref,
    loss_ref, qgrad_ref, g1_ref, g2_ref,
    q_all, meta_in, emb_all, flags_all, scores, coeffs, stats_all,
    e_acc, e_recv_c, e_recv_x, q_acc, q_recv_y, q_recv_z,
    pre_act, hidden,
    a_acc, a_recv_c, a_recv_x, a_recv_y, a_recv_z, a_out,
    b_acc, b_recv_c, b_recv_x, b_recv_y, b_recv_z, b_out,
    send_sems, recv_sems,
):
    nq, ni, grad_scale = shape
    gx, gz = ni // 2, nq // 2
    q, i = lax.axis_index("query"), lax.axis_index("item")
    core, x = lax.rem(i, 2), lax.div(i, 2)
    y, z = lax.rem(q, 2), lax.div(q, 2)
    q_rows, width = query_ref.shape
    n_q = nq * q_rows
    block = tokens_ref.shape[0]
    used = [0]

    def send(src, dst, peer):
        slot = used[0]
        used[0] += 1
        copy = pltpu.make_async_remote_copy(
            src_ref=src, dst_ref=dst, send_sem=send_sems.at[slot], recv_sem=recv_sems.at[slot],
            device_id=peer, device_id_type=pl.DeviceIdType.MESH,
        )
        copy.start()
        return copy

    def finish(copies):
        for copy in copies:
            copy.wait()

    axes = {
        "core": (2, core, lambda t: {"item": x * 2 + t}),
        "x": (gx, x, lambda t: {"item": t * 2 + core}),
        "y": (2, y, lambda t: {"query": z * 2 + t}),
        "z": (gz, z, lambda t: {"query": t * 2 + y}),
    }

    def reduce_start(acc, recv, base, size, axis):
        group, own, peer = axes[axis]
        copies = []
        for k in range(1, group):
            there = lax.rem(own + k, group)
            copies.append(
                send(acc.at[rows(base + there * size, size)], recv.at[rows((k - 1) * size, size)], peer(there))
            )
        return copies

    def reduce_finish(copies, acc, recv, base, size, axis):
        group, own, _ = axes[axis]
        finish(copies)
        here = rows(base + own * size, size)
        total = acc[here, :]
        for k in range(1, group):
            total = total + recv[rows((k - 1) * size, size), :]
        acc[here, :] = total
        return base + own * size

    def gather_start(buf, base, size, axis):
        group, own, peer = axes[axis]
        here = buf.at[rows(base + own * size, size)]
        return [send(here, here, peer(lax.rem(own + k, group))) for k in range(1, group)]

    barrier = pltpu.get_barrier_semaphore()
    for k in range(1, nq):
        pl.semaphore_signal(
            barrier, inc=1, device_id={"query": lax.rem(q + k, nq)}, device_id_type=pl.DeviceIdType.MESH
        )
    for k in range(1, ni):
        pl.semaphore_signal(
            barrier, inc=1, device_id={"item": lax.rem(i + k, ni)}, device_id_type=pl.DeviceIdType.MESH
        )
    pl.semaphore_wait(barrier, nq + ni - 2)

    q_pos = y * gz + z
    copies = []
    for k in range(1, nq):
        there = lax.rem(q + k, nq)
        copies.append(send(meta_ref.at[there], meta_in.at[k], {"query": there}))
        copies.append(send(query_ref, q_all.at[rows(q_pos * q_rows, q_rows)], {"query": there}))
    q_all[rows(q_pos * q_rows, q_rows), :] = query_ref[...]
    meta_in[0] = meta_ref[q]

    tokens = tokens_ref[...]
    pre = dot(tokens, w1_ref[...], (1, 0))
    pre_act[...] = pre
    hidden[...] = jax.nn.silu(pre).astype(BF16)
    i_pos = core * gx + x
    emb_all[rows(i_pos * block, block), :] = dot(hidden[...], w2_ref[...], (1, 0)).astype(BF16)

    finish(copies)
    flags = meta_in[0]
    for k in range(1, nq):
        flags = flags + meta_in[k]
    meta_rows = flags.shape[0]
    flags_all[rows(i_pos * meta_rows, meta_rows), :] = flags
    wanted = flags[ni : ni + 1, :]

    finish(
        gather_start(emb_all, core * gx * block, block, "x")
        + gather_start(flags_all, core * gx * meta_rows, meta_rows, "x")
    )
    finish(
        gather_start(emb_all, 0, gx * block, "core") + gather_start(flags_all, 0, gx * meta_rows, "core")
    )

    def located(p):
        item = lax.rem(p, gx) * 2 + lax.div(p, gx)
        first = (item * nq + q) * block
        ids = lax.broadcasted_iota(jnp.int32, (block, n_q), 0)
        hit = ids == (wanted - first)
        live = flags_all[pl.ds(p * meta_rows + i, 1), :] > 0
        return hit, live

    def score_block(p, carried):
        top, total, positive = carried
        hit, live = located(p)
        s = 0.25 * dot(emb_all[rows(p * block, block), :], q_all[...], (1, 1))
        scores[rows(p * block, block), :] = s
        here = jnp.max(s, axis=0, keepdims=True)
        added = jnp.sum(jnp.exp(s - here), axis=0, keepdims=True)
        positive = positive + jnp.sum(jnp.where(hit, s, 0.0), axis=0, keepdims=True)
        here = jnp.where(live, here, -1e30)
        new_top = jnp.maximum(top, here)
        total = total * jnp.exp(top - new_top) + jnp.where(live, added * jnp.exp(here - new_top), 0.0)
        return new_top, total, positive

    start = (jnp.full((1, n_q), -1e30, F32), jnp.zeros((1, n_q), F32), jnp.zeros((1, n_q), F32))
    top, total, positive = lax.fori_loop(0, ni, score_block, start)
    stats_all[0] = jnp.concatenate([top, total, positive, jnp.zeros((5, n_q), F32)], axis=0)
    finish([
        send(stats_all.at[0], stats_all.at[k], {"query": lax.rem(q + k, nq)}) for k in range(1, nq)
    ])
    top = stats_all[0, 0:1, :]
    for k in range(1, nq):
        top = jnp.maximum(top, stats_all[k, 0:1, :])
    total = jnp.zeros((1, n_q), F32)
    positive = jnp.zeros((1, n_q), F32)
    for k in range(nq):
        total = total + stats_all[k, 1:2, :] * jnp.exp(stats_all[k, 0:1, :] - top)
        positive = positive + stats_all[k, 2:3, :]
    log_norm = top + jnp.log(total)
    loss_ref[...] = log_norm - positive

    def grad_block(p, carried):
        hit, live = located(p)
        s = scores[rows(p * block, block), :]
        weights = jnp.where(live, jnp.exp(s - log_norm), 0.0)
        c = (weights - hit.astype(F32)).astype(BF16)
        coeffs[rows(p * block, block), :] = c
        e_acc[rows(p * block, block), :] = 0.25 * dot(c, q_all[...], (1, 0))
        return carried

    lax.fori_loop(0, ni, grad_block, 0)
    e_copies = reduce_start(e_acc, e_recv_c, 0, gx * block, "core")
    q_acc[...] = 0.25 * dot(coeffs[...], emb_all[...], (0, 0))
    q_copies = reduce_start(q_acc, q_recv_y, 0, gz * q_rows, "y")
    e_base = reduce_finish(e_copies, e_acc, e_recv_c, 0, gx * block, "core")
    e_copies = reduce_start(e_acc, e_recv_x, e_base, block, "x")
    e_base = reduce_finish(e_copies, e_acc, e_recv_x, e_base, block, "x")
    own_grad = e_acc[rows(e_base, block), :].astype(BF16)

    second = dot(hidden[...], own_grad, (0, 0))
    hid = second.shape[0]
    b_rows, a_rows = b_acc.shape[0], a_acc.shape[0]
    din = tokens.shape[1]
    for j in range(width // 128):
        b_acc[j * hid : (j + 1) * hid, :] = second[:, j * 128 : (j + 1) * 128]
    b_size = b_rows // 2
    b_copies = reduce_start(b_acc, b_recv_c, 0, b_size, "core")
    hid_grad = dot(own_grad, w2_ref[...], (1, 1))
    pre = pre_act[...]
    sig = jax.nn.sigmoid(pre)
    pre_grad = (hid_grad * sig * (1.0 + pre * (1.0 - sig))).astype(BF16)
    first = dot(tokens, pre_grad, (0, 0))
    for j in range(hid // 128):
        a_acc[j * din : (j + 1) * din, :] = first[:, j * 128 : (j + 1) * 128]
    a_size = a_rows // 2
    a_copies = reduce_start(a_acc, a_recv_c, 0, a_size, "core")

    q_base = reduce_finish(q_copies, q_acc, q_recv_y, 0, gz * q_rows, "y")
    b_base = reduce_finish(b_copies, b_acc, b_recv_c, 0, b_size, "core")
    b_size = b_size // 2
    b_copies = reduce_start(b_acc, b_recv_y, b_base, b_size, "y")
    a_base = reduce_finish(a_copies, a_acc, a_recv_c, 0, a_size, "core")
    a_size = a_size // gx
    a_copies = reduce_start(a_acc, a_recv_x, a_base, a_size, "x")
    q_copies = reduce_start(q_acc, q_recv_z, q_base, q_rows, "z")
    b_base = reduce_finish(b_copies, b_acc, b_recv_y, b_base, b_size, "y")
    b_size = b_size // gx
    b_copies = reduce_start(b_acc, b_recv_x, b_base, b_size, "x")
    q_base = reduce_finish(q_copies, q_acc, q_recv_z, q_base, q_rows, "z")
    qgrad_ref[...] = q_acc[rows(q_base, q_rows), :]
    a_base = reduce_finish(a_copies, a_acc, a_recv_x, a_base, a_size, "x")
    a_size = a_size // 2
    a_copies = reduce_start(a_acc, a_recv_y, a_base, a_size, "y")
    b_base = reduce_finish(b_copies, b_acc, b_recv_x, b_base, b_size, "x")
    b_size = b_size // gz
    b_copies = reduce_start(b_acc, b_recv_z, b_base, b_size, "z")
    a_base = reduce_finish(a_copies, a_acc, a_recv_y, a_base, a_size, "y")
    a_size = a_size // gz
    a_copies = reduce_start(a_acc, a_recv_z, a_base, a_size, "z")

    b_base = reduce_finish(b_copies, b_acc, b_recv_z, b_base, b_size, "z")
    b_out[rows(b_base, b_size), :] = (b_acc[rows(b_base, b_size), :] * grad_scale).astype(b_out.dtype)
    b_base = b_base - z * b_size
    b_copies = gather_start(b_out, b_base, b_size, "z")
    a_base = reduce_finish(a_copies, a_acc, a_recv_z, a_base, a_size, "z")
    a_out[rows(a_base, a_size), :] = (a_acc[rows(a_base, a_size), :] * grad_scale).astype(a_out.dtype)
    a_base = a_base - z * a_size
    a_copies = gather_start(a_out, a_base, a_size, "z")
    finish(b_copies)
    b_size = b_size * gz
    b_base = b_base - x * b_size
    b_copies = gather_start(b_out, b_base, b_size, "x")
    finish(a_copies)
    a_size = a_size * gz
    a_base = a_base - y * a_size
    a_copies = gather_start(a_out, a_base, a_size, "y")
    finish(b_copies)
    b_size = b_size * gx
    b_base = b_base - y * b_size
    b_copies = gather_start(b_out, b_base, b_size, "y")
    finish(a_copies)
    a_size = a_size * 2
    a_base = a_base - x * a_size
    a_copies = gather_start(a_out, a_base, a_size, "x")
    finish(b_copies)
    b_copies = gather_start(b_out, 0, b_rows // 2, "core")
    finish(b_copies)
    for j in range(width // 128):
        g2_ref[:, j * 128 : (j + 1) * 128] = b_out[j * hid : (j + 1) * hid, :].astype(F32)
    finish(a_copies)
    a_copies = gather_start(a_out, 0, a_rows // 2, "core")
    finish(a_copies)
    for j in range(hid // 128):
        g1_ref[:, j * 128 : (j + 1) * 128] = a_out[j * din : (j + 1) * din, :].astype(F32)


def on_device(query_emb, targets, eligible_tiles, item_feats, w_first, w_second):
    q_rows, width = query_emb.shape
    ni, nq = lax.axis_size("item"), lax.axis_size("query")
    gx, gz = ni // 2, nq // 2
    i, q = lax.axis_index("item"), lax.axis_index("query")
    tokens = item_feats.reshape(item_feats.shape[1], item_feats.shape[2])
    block, din = tokens.shape
    hid = w_first.shape[1]
    n_q = nq * q_rows
    q_pos = (q % 2) * gz + q // 2
    meta_rows = -(-(ni + 1) // 8) * 8
    own = lax.dynamic_slice_in_dim(targets, i * q_rows, q_rows, 0)
    flags = jnp.broadcast_to((eligible_tiles > 0).astype(jnp.int32).T[:, :, None], (nq, ni, n_q))
    mine = (jnp.arange(n_q, dtype=jnp.int32) // q_rows == q_pos).astype(jnp.int32)
    meta = jnp.concatenate(
        [
            flags,
            jnp.broadcast_to(jnp.tile(own, nq)[None, None, :], (nq, 1, n_q)),
            jnp.zeros((nq, meta_rows - ni - 1, n_q), jnp.int32),
        ],
        axis=1,
    ) * mine[None, None, :]

    a_rows, b_rows = din * hid // 128, hid * width // 128
    a_dtype = BF16 if a_rows // (nq * ni) % 16 == 0 else F32
    b_dtype = BF16 if b_rows // (nq * ni) % 16 == 0 else F32
    n_copies = 2 * (nq - 1) + 2 * gx + nq - 1 + gx + gz + 4 * (2 + gx - 1 + gz - 1) + 8
    vmem = pltpu.VMEM
    loss, query_grad, g1, g2 = pl.pallas_call(
        functools.partial(window_kernel, (nq, ni, 1.0 / math.sqrt(block * nq * ni))),
        out_shape=(
            jax.ShapeDtypeStruct((1, n_q), F32),
            jax.ShapeDtypeStruct((q_rows, width), F32),
            jax.ShapeDtypeStruct((din, hid), F32),
            jax.ShapeDtypeStruct((hid, width), F32),
        ),
        in_specs=[pl.BlockSpec(memory_space=vmem)] * 5,
        out_specs=(pl.BlockSpec(memory_space=vmem),) * 4,
        scratch_shapes=[
            vmem((n_q, width), BF16),
            vmem((nq, meta_rows, n_q), jnp.int32),
            vmem((ni * block, width), BF16),
            vmem((ni * meta_rows, n_q), jnp.int32),
            vmem((ni * block, n_q), F32),
            vmem((ni * block, n_q), BF16),
            vmem((nq, 8, n_q), F32),
            vmem((ni * block, width), F32),
            vmem((gx * block, width), F32),
            vmem((max(gx - 1, 1) * block, width), F32),
            vmem((n_q, width), F32),
            vmem((gz * q_rows, width), F32),
            vmem((max(gz - 1, 1) * q_rows, width), F32),
            vmem((block, hid), F32),
            vmem((block, hid), BF16),
            vmem((a_rows, 128), F32),
            vmem((a_rows // 2, 128), F32),
            vmem((a_rows // 2 // gx * (gx - 1), 128), F32),
            vmem((a_rows // 4 // gx, 128), F32),
            vmem((a_rows // 4 // gx // gz * (gz - 1), 128), F32),
            vmem((a_rows, 128), a_dtype),
            vmem((b_rows, 128), F32),
            vmem((b_rows // 2, 128), F32),
            vmem((b_rows // 4 // gx * (gx - 1), 128), F32),
            vmem((b_rows // 4, 128), F32),
            vmem((b_rows // 4 // gx // gz * (gz - 1), 128), F32),
            vmem((b_rows, 128), b_dtype),
            pltpu.SemaphoreType.DMA((n_copies,)),
            pltpu.SemaphoreType.DMA((n_copies,)),
        ],
        compiler_params=pltpu.CompilerParams(
            collective_id=0, has_side_effects=True, vmem_limit_bytes=58 * 2**20
        ),
        name="loss_window",
    )(query_emb, meta, tokens, w_first, w_second)
    loss = lax.dynamic_slice_in_dim(loss.reshape(n_q), q_pos * q_rows, q_rows, 0)
    return (loss, query_grad, g1, g2)


def solution(mesh):
    return jax.shard_map(
        on_device,
        mesh=mesh,
        in_specs=(
            P(("query", "item"), None),
            P("query"),
            P("query", "item"),
            P("item", "query", None),
            P(),
            P(),
        ),
        out_specs=(P(("query", "item")), P(("query", "item"), None), P(), P()),
        check_vma=False,
    )
```

```python
import functools
import math

import jax
import jax.numpy as jnp
from jax import lax
from jax.experimental import pallas as pl
from jax.experimental.pallas import tpu as pltpu
from jax.sharding import PartitionSpec as P

F32 = jnp.float32
BF16 = jnp.bfloat16


def dot(a, b, contract):
    return lax.dot_general(a, b, ((contract[:1], contract[1:]), ((), ())), preferred_element_type=F32)


def rows(start, size):
    return pl.ds(pl.multiple_of(start, math.gcd(size, 256)), size)


def window_kernel(
    shape,
    query_ref, raw_ref, tokens_ref, w1_ref, w2_ref,
    loss_ref, qgrad_ref, a_out, b_out,
    q_all, raw_in, meta_in, emb_all, flags_all, scores, coeffs, stats_all,
    e_acc, e_recv_c, e_recv_x, q_acc, q_recv_y, q_recv_z,
    pre_act, hidden, a_acc, b_acc, core_recv, x_recv, y_recv, z_recv,
    send_sems, recv_sems,
):
    nq, ni, grad_scale = shape
    gx, gz = ni // 2, nq // 2
    q, i = lax.axis_index("query"), lax.axis_index("item")
    core, x = lax.rem(i, 2), lax.div(i, 2)
    y, z = lax.rem(q, 2), lax.div(q, 2)
    q_rows, width = query_ref.shape
    n_q = nq * q_rows
    block = tokens_ref.shape[0]
    used = [0]

    def send(src, dst, peer):
        slot = used[0]
        used[0] += 1
        copy = pltpu.make_async_remote_copy(
            src_ref=src, dst_ref=dst, send_sem=send_sems.at[slot], recv_sem=recv_sems.at[slot],
            device_id=peer, device_id_type=pl.DeviceIdType.MESH,
        )
        copy.start()
        return copy

    def finish(copies):
        for copy in copies:
            copy.wait()

    axes = {
        "core": (2, core, lambda t: {"item": x * 2 + t}),
        "x": (gx, x, lambda t: {"item": t * 2 + core}),
        "y": (2, y, lambda t: {"query": z * 2 + t}),
        "z": (gz, z, lambda t: {"query": t * 2 + y}),
    }

    def reduce_start(acc, recv, base, size, axis):
        group, own, peer = axes[axis]
        copies = []
        for k in range(1, group):
            there = lax.rem(own + k, group)
            copies.append(
                send(acc.at[rows(base + there * size, size)], recv.at[rows((k - 1) * size, size)], peer(there))
            )
        return copies

    def reduce_finish(copies, acc, recv, base, size, axis):
        group, own, _ = axes[axis]
        finish(copies)
        here = rows(base + own * size, size)
        total = acc[here, :]
        for k in range(1, group):
            total = total + recv[rows((k - 1) * size, size), :]
        acc[here, :] = total
        return base + own * size

    def gather_start(buf, base, size, axis):
        group, own, peer = axes[axis]
        here = buf.at[rows(base + own * size, size)]
        return [send(here, here, peer(lax.rem(own + k, group))) for k in range(1, group)]

    barrier = pltpu.get_barrier_semaphore()
    for k in range(1, nq):
        pl.semaphore_signal(
            barrier, inc=1, device_id={"query": lax.rem(q + k, nq)}, device_id_type=pl.DeviceIdType.MESH
        )
    for k in range(1, ni):
        pl.semaphore_signal(
            barrier, inc=1, device_id={"item": lax.rem(i + k, ni)}, device_id_type=pl.DeviceIdType.MESH
        )
    pl.semaphore_wait(barrier, nq + ni - 2)

    q_pos = y * gz + z
    query_copies = []
    for k in range(1, nq):
        there = lax.rem(q + k, nq)
        query_copies.append(send(query_ref, q_all.at[rows(q_pos * q_rows, q_rows)], {"query": there}))
    raw_copies = [send(raw_ref, raw_in.at[i], {"item": lax.rem(i + k, ni)}) for k in range(1, ni)]
    q_all[rows(q_pos * q_rows, q_rows), :] = query_ref[...]
    raw_in[i] = raw_ref[...]
    tokens = tokens_ref[...]
    pre = dot(tokens, w1_ref[...], (1, 0))
    pre_act[...] = pre
    finish(raw_copies)
    meta_rows = raw_ref.shape[0]
    parts = [raw_in[t, pl.ds(i, 1), :] for t in range(ni)] + [raw_ref[ni : ni + 1, :]]
    if meta_rows > ni + 1:
        parts.append(jnp.zeros((meta_rows - ni - 1, 128), jnp.int32))
    meta_in[q_pos] = jnp.concatenate(parts, axis=0)
    for k in range(1, nq):
        query_copies.append(send(meta_in.at[q_pos], meta_in.at[q_pos], {"query": lax.rem(q + k, nq)}))
    hidden[...] = jax.nn.silu(pre).astype(BF16)
    i_pos = core * gx + x
    emb_all[rows(i_pos * block, block), :] = dot(hidden[...], w2_ref[...], (1, 0)).astype(BF16)

    finish(gather_start(emb_all, core * gx * block, block, "x"))
    finish(gather_start(emb_all, 0, gx * block, "core"))

    finish(query_copies)
    lane = lax.broadcasted_iota(jnp.int32, (meta_rows, 128), 1)
    per = 128 // q_rows
    want_tiles, flag_tiles = [], []
    for t in range(nq // per):
        want = jnp.zeros((1, 128), jnp.int32)
        flag = jnp.zeros((meta_rows, 128), F32)
        for h in range(per):
            sent = meta_in[t * per + h]
            want = want + sent[ni : ni + 1, :]
            column = jnp.sum(jnp.where(lane == q, sent, 0).astype(F32), axis=1, keepdims=True)
            inside = (lane >= h * q_rows) & (lane < (h + 1) * q_rows)
            flag = flag + jnp.where(inside, column, 0.0)
        want_tiles.append(want)
        flag_tiles.append(flag)
    wanted = jnp.concatenate(want_tiles, axis=1)
    flags_all[...] = jnp.concatenate(flag_tiles, axis=1)

    def located(p):
        item = lax.rem(p, gx) * 2 + lax.div(p, gx)
        first = (item * nq + q) * block
        ids = lax.broadcasted_iota(jnp.int32, (block, n_q), 0)
        hit = ids == (wanted - first)
        live = flags_all[pl.ds(item, 1), :] > 0.5
        return hit, live

    def score_block(p, carried):
        top, total, positive = carried
        hit, live = located(p)
        s = 0.25 * dot(emb_all[rows(p * block, block), :], q_all[...], (1, 1))
        scores[rows(p * block, block), :] = s
        here = jnp.max(s, axis=0, keepdims=True)
        added = jnp.sum(jnp.exp(s - here), axis=0, keepdims=True)
        positive = positive + jnp.sum(jnp.where(hit, s, 0.0), axis=0, keepdims=True)
        here = jnp.where(live, here, -1e30)
        new_top = jnp.maximum(top, here)
        total = total * jnp.exp(top - new_top) + jnp.where(live, added * jnp.exp(here - new_top), 0.0)
        return new_top, total, positive

    start = (jnp.full((1, n_q), -1e30, F32), jnp.zeros((1, n_q), F32), jnp.zeros((1, n_q), F32))
    top, total, positive = lax.fori_loop(0, ni, score_block, start)
    stats_all[0] = jnp.concatenate([top, total, positive, jnp.zeros((5, n_q), F32)], axis=0)
    finish([
        send(stats_all.at[0], stats_all.at[k], {"query": lax.rem(q + k, nq)}) for k in range(1, nq)
    ])
    top = stats_all[0, 0:1, :]
    for k in range(1, nq):
        top = jnp.maximum(top, stats_all[k, 0:1, :])
    total = jnp.zeros((1, n_q), F32)
    positive = jnp.zeros((1, n_q), F32)
    for k in range(nq):
        total = total + stats_all[k, 1:2, :] * jnp.exp(stats_all[k, 0:1, :] - top)
        positive = positive + stats_all[k, 2:3, :]
    log_norm = top + jnp.log(total)
    loss_ref[...] = log_norm - positive

    def grad_block(p, carried):
        hit, live = located(p)
        s = scores[rows(p * block, block), :]
        weights = jnp.where(live, jnp.exp(s - log_norm), 0.0)
        c = (weights - hit.astype(F32)).astype(BF16)
        coeffs[rows(p * block, block), :] = c
        e_acc[rows(p * block, block), :] = 0.25 * dot(c, q_all[...], (1, 0))
        return carried

    lax.fori_loop((1 - core) * gx, (2 - core) * gx, grad_block, 0)
    e_copies = reduce_start(e_acc, e_recv_c, 0, gx * block, "core")
    lax.fori_loop(core * gx, (core + 1) * gx, grad_block, 0)
    e_base = reduce_finish(e_copies, e_acc, e_recv_c, 0, gx * block, "core")
    e_copies = reduce_start(e_acc, e_recv_x, e_base, block, "x")
    q_acc[...] = 0.25 * dot(coeffs[...], emb_all[...], (0, 0))
    q_copies = reduce_start(q_acc, q_recv_y, 0, gz * q_rows, "y")
    e_base = reduce_finish(e_copies, e_acc, e_recv_x, e_base, block, "x")
    own_grad = e_acc[rows(e_base, block), :].astype(BF16)

    hid, din = w2_ref.shape[0], tokens.shape[1]
    part = b_acc.shape[0]
    chains = [
        {"acc": a_acc, "out": a_out, "first": 0, "order": ("core", "x", "y", "z")},
        {"acc": a_acc, "out": a_out, "first": part, "order": ("core", "y", "x", "z")},
        {"acc": b_acc, "out": b_out, "first": 0, "order": ("core", "z", "x", "y")},
    ]
    landing = {"core": core_recv, "x": x_recv, "y": y_recv, "z": z_recv}

    def descend(n):
        chain = chains[n]
        level = chain.setdefault("level", 0)
        if level == 0:
            chain["base"], chain["size"] = chain["first"], part
        else:
            chain["base"] = reduce_finish(
                chain["copies"], chain["acc"], landing[chain["order"][level - 1]].at[n],
                chain["base"], chain["size"], chain["order"][level - 1],
            )
        if level < 4:
            axis = chain["order"][level]
            chain["size"] = chain["size"] // axes[axis][0]
            chain["copies"] = reduce_start(
                chain["acc"], landing[axis].at[n], chain["base"], chain["size"], axis
            )
            chain["level"] = level + 1
        else:
            here = rows(chain["base"], chain["size"])
            chain["out"][here, :] = (chain["acc"][here, :] * grad_scale).astype(chain["out"].dtype)
            chain["copies"] = []

    def ascend(n):
        chain = chains[n]
        finish(chain["copies"])
        level = chain["level"] - 1
        chain["level"] = level
        if level < 0:
            return
        group, own, _ = axes[chain["order"][level]]
        chain["base"] = chain["base"] - own * chain["size"]
        chain["copies"] = gather_start(
            chain["out"], chain["base"], chain["size"], chain["order"][level]
        )
        chain["size"] = chain["size"] * group

    second = dot(hidden[...], own_grad, (0, 0))
    for j in range(width // 128):
        b_acc[j * hid : (j + 1) * hid, :] = second[:, j * 128 : (j + 1) * 128]
    descend(2)
    hid_grad = dot(own_grad, w2_ref[...], (1, 1))
    pre = pre_act[...]
    sig = jax.nn.sigmoid(pre)
    pre_grad = (hid_grad * sig * (1.0 + pre * (1.0 - sig))).astype(BF16)
    half = hid // 2
    for n in range(2):
        first = dot(tokens, pre_grad[:, n * half : (n + 1) * half], (0, 0))
        for j in range(half // 128):
            start_row = n * part + j * din
            a_acc[start_row : start_row + din, :] = first[:, j * 128 : (j + 1) * 128]
        descend(n)
        if n == 0:
            descend(2)
            q_base = reduce_finish(q_copies, q_acc, q_recv_y, 0, gz * q_rows, "y")
            q_copies = reduce_start(q_acc, q_recv_z, q_base, q_rows, "z")
    for n in (0, 1, 0, 1, 2):
        descend(n)
    q_base = reduce_finish(q_copies, q_acc, q_recv_z, q_base, q_rows, "z")
    qgrad_ref[...] = q_acc[rows(q_base, q_rows), :]
    for n in (0, 1, 2):
        descend(n)
    descend(2)
    ascend(2)
    for n in (0, 1):
        descend(n)
        ascend(n)
    for n in (2, 0, 1, 2, 0, 1, 0, 1, 2, 0, 1, 2):
        ascend(n)


def on_device(query_emb, targets, eligible_tiles, item_feats, w_first, w_second):
    q_rows, width = query_emb.shape
    ni, nq = lax.axis_size("item"), lax.axis_size("query")
    gx, gz = ni // 2, nq // 2
    i, q = lax.axis_index("item"), lax.axis_index("query")
    tokens = item_feats.reshape(item_feats.shape[1], item_feats.shape[2])
    block, din = tokens.shape
    hid = w_first.shape[1]
    n_q = nq * q_rows
    q_pos = (q % 2) * gz + q // 2
    meta_rows = -(-(ni + 1) // 8) * 8
    per = 128 // q_rows
    own = lax.dynamic_slice_in_dim(targets, i * q_rows, q_rows, 0)
    mine = jnp.arange(128, dtype=jnp.int32) // q_rows == q_pos % per
    flags = jnp.pad((eligible_tiles > 0).astype(jnp.int32), ((0, meta_rows - ni), (0, 128 - nq)))
    at_row = jnp.arange(meta_rows, dtype=jnp.int32)[:, None] == ni
    raw = jnp.where(at_row, jnp.where(mine, jnp.tile(own, per), 0)[None, :], flags)

    a_rows, b_rows = din * hid // 128, hid * width // 128
    part = b_rows
    out_dtype = BF16 if part // (nq * ni) % 16 == 0 else F32
    n_copies = 3 * (nq - 1) + (ni - 1) + 2 * gx + gx + gz + 3 * 2 * (2 + gx - 1 + gz - 1)
    vmem = pltpu.VMEM
    loss, query_grad, g1, g2 = pl.pallas_call(
        functools.partial(window_kernel, (nq, ni, 1.0 / math.sqrt(block * nq * ni))),
        out_shape=(
            jax.ShapeDtypeStruct((1, n_q), F32),
            jax.ShapeDtypeStruct((q_rows, width), F32),
            jax.ShapeDtypeStruct((a_rows, 128), out_dtype),
            jax.ShapeDtypeStruct((b_rows, 128), out_dtype),
        ),
        in_specs=[pl.BlockSpec(memory_space=vmem)] * 5,
        out_specs=(pl.BlockSpec(memory_space=vmem),) * 4,
        scratch_shapes=[
            vmem((n_q, width), BF16),
            vmem((ni, meta_rows, 128), jnp.int32),
            vmem((nq, meta_rows, 128), jnp.int32),
            vmem((ni * block, width), BF16),
            vmem((meta_rows, n_q), F32),
            vmem((ni * block, n_q), F32),
            vmem((ni * block, n_q), BF16),
            vmem((nq, 8, n_q), F32),
            vmem((ni * block, width), F32),
            vmem((gx * block, width), F32),
            vmem((max(gx - 1, 1) * block, width), F32),
            vmem((n_q, width), F32),
            vmem((gz * q_rows, width), F32),
            vmem((max(gz - 1, 1) * q_rows, width), F32),
            vmem((block, hid), F32),
            vmem((block, hid), BF16),
            vmem((a_rows, 128), F32),
            vmem((b_rows, 128), F32),
            vmem((3, part // 2, 128), F32),
            vmem((3, part // 2, 128), F32),
            vmem((3, part // 4, 128), F32),
            vmem((3, part // 2, 128), F32),
            pltpu.SemaphoreType.DMA((n_copies,)),
            pltpu.SemaphoreType.DMA((n_copies,)),
        ],
        compiler_params=pltpu.CompilerParams(
            collective_id=0, has_side_effects=True, vmem_limit_bytes=58 * 2**20
        ),
        name="loss_window",
    )(query_emb, raw, tokens, w_first, w_second)
    loss = lax.dynamic_slice_in_dim(loss.reshape(n_q), q_pos * q_rows, q_rows, 0)
    g1 = g1.reshape(hid // 128, din, 128).transpose(1, 0, 2).reshape(din, hid).astype(F32)
    g2 = g2.reshape(width // 128, hid, 128).transpose(1, 0, 2).reshape(hid, width).astype(F32)
    return (loss, query_grad, g1, g2)


def solution(mesh):
    return jax.shard_map(
        on_device,
        mesh=mesh,
        in_specs=(
            P(("query", "item"), None),
            P("query"),
            P("query", "item"),
            P("item", "query", None),
            P(),
            P(),
        ),
        out_specs=(P(("query", "item")), P(("query", "item"), None), P(), P()),
        check_vma=False,
    )
```

```python
import functools
import math

import jax
import jax.numpy as jnp
from jax import lax
from jax.experimental import pallas as pl
from jax.experimental.pallas import tpu as pltpu
from jax.sharding import PartitionSpec as P

F32 = jnp.float32
BF16 = jnp.bfloat16


def dot(a, b, contract):
    return lax.dot_general(a, b, ((contract[:1], contract[1:]), ((), ())), preferred_element_type=F32)


def rows(start, size):
    return pl.ds(pl.multiple_of(start, math.gcd(size, 256)), size)


def window_kernel(
    shape,
    query_ref, targets_ref, flags_ref, tokens_hbm, w1_hbm, w2_hbm,
    loss_ref, qgrad_ref, a_out, b_out,
    tokens_ref, w1_ref, w2_ref, q_all, raw_in, meta_in, emb_all, flags_all, scores, coeffs, stats_all,
    e_acc, e_recv_c, e_recv_x, q_acc, q_recv_y, q_recv_l, q_recv_h,
    pre_act, hidden, a_acc, b_acc, core_recv, x_recv, y_recv, l_recv, h_recv,
    send_sems, recv_sems, load_sems,
):
    nq, ni, grad_scale = shape
    gx, gz = ni // 2, nq // 2
    q, i = lax.axis_index("query"), lax.axis_index("item")
    core, x = lax.rem(i, 2), lax.div(i, 2)
    y, z = lax.rem(q, 2), lax.div(q, 2)
    zl, zh = lax.rem(z, 2), lax.div(z, 2)
    gh = gz // 2
    q_rows, width = query_ref.shape
    n_q = nq * q_rows
    block = tokens_ref.shape[0]
    used = [0]
    loads = [
        pltpu.make_async_copy(src, dst, load_sems.at[n])
        for n, (src, dst) in enumerate(((tokens_hbm, tokens_ref), (w1_hbm, w1_ref), (w2_hbm, w2_ref)))
    ]
    for load in loads:
        load.start()

    def send(src, dst, peer):
        slot = used[0]
        used[0] += 1
        copy = pltpu.make_async_remote_copy(
            src_ref=src, dst_ref=dst, send_sem=send_sems.at[slot], recv_sem=recv_sems.at[slot],
            device_id=peer, device_id_type=pl.DeviceIdType.MESH,
        )
        copy.start()
        return copy

    def finish(copies):
        for copy in copies:
            copy.wait()

    axes = {
        "core": (2, core, lambda t: {"item": x * 2 + t}),
        "x": (gx, x, lambda t: {"item": t * 2 + core}),
        "y": (2, y, lambda t: {"query": z * 2 + t}),
        "zl": (2, zl, lambda t: {"query": (zh * 2 + t) * 2 + y}),
        "zh": (gh, zh, lambda t: {"query": (t * 2 + zl) * 2 + y}),
    }

    def reduce_start(acc, recv, base, size, axis):
        group, own, peer = axes[axis]
        copies = []
        for k in range(1, group):
            there = lax.rem(own + k, group)
            copies.append(
                send(acc.at[rows(base + there * size, size)], recv.at[rows((k - 1) * size, size)], peer(there))
            )
        return copies

    def reduce_finish(copies, acc, recv, base, size, axis):
        group, own, _ = axes[axis]
        finish(copies)
        here = rows(base + own * size, size)
        total = acc[here, :]
        for k in range(1, group):
            total = total + recv[rows((k - 1) * size, size), :]
        acc[here, :] = total
        return base + own * size

    def gather_start(buf, base, size, axis):
        group, own, peer = axes[axis]
        here = buf.at[rows(base + own * size, size)]
        return [send(here, here, peer(lax.rem(own + k, group))) for k in range(1, group)]

    barrier = pltpu.get_barrier_semaphore()
    for k in range(1, nq):
        pl.semaphore_signal(
            barrier, inc=1, device_id={"query": lax.rem(q + k, nq)}, device_id_type=pl.DeviceIdType.MESH
        )
    for k in range(1, ni):
        pl.semaphore_signal(
            barrier, inc=1, device_id={"item": lax.rem(i + k, ni)}, device_id_type=pl.DeviceIdType.MESH
        )
    pl.semaphore_wait(barrier, nq + ni - 2)

    q_pos = (y * 2 + zl) * gh + zh
    query_copies = []
    for k in range(1, nq):
        there = lax.rem(q + k, nq)
        query_copies.append(send(query_ref, q_all.at[rows(q_pos * q_rows, q_rows)], {"query": there}))
    per = 128 // q_rows
    meta_rows = raw_in.shape[1]
    raw_in[i] = jnp.zeros((meta_rows, 128), jnp.int32)
    raw_in[i, 0:ni, 0:nq] = (flags_ref[...] > 0).astype(jnp.int32)
    raw_copies = [send(raw_in.at[i], raw_in.at[i], {"item": lax.rem(i + k, ni)}) for k in range(1, ni)]
    q_all[rows(q_pos * q_rows, q_rows), :] = query_ref[...]
    lane_row = lax.broadcasted_iota(jnp.int32, (1, 128), 1)
    first_lane = pl.multiple_of(lax.div(i, per) * 128, 128)
    found = targets_ref[:, pl.ds(first_lane, 128)]
    shift = lax.rem(q_pos - i + per * nq * ni, per)
    moved = found
    for h in range(1, per):
        moved = jnp.where(shift == h, pltpu.roll(found, h * q_rows, 1), moved)
    inside = lax.div(lane_row, q_rows) == lax.rem(q_pos, per)
    own_targets = jnp.where(inside, moved, 0)
    loads[0].wait()
    loads[1].wait()
    tokens = tokens_ref[...]
    pre = dot(tokens, w1_ref[...], (1, 0))
    pre_act[...] = pre
    finish(raw_copies)
    parts = [raw_in[t, pl.ds(i, 1), :] for t in range(ni)] + [own_targets]
    if meta_rows > ni + 1:
        parts.append(jnp.zeros((meta_rows - ni - 1, 128), jnp.int32))
    meta_in[q_pos] = jnp.concatenate(parts, axis=0)
    for k in range(1, nq):
        query_copies.append(send(meta_in.at[q_pos], meta_in.at[q_pos], {"query": lax.rem(q + k, nq)}))
    loads[2].wait()
    hidden[...] = jax.nn.silu(pre).astype(BF16)
    i_pos = core * gx + x
    emb_all[rows(i_pos * block, block), :] = dot(hidden[...], w2_ref[...], (1, 0)).astype(BF16)

    finish(gather_start(emb_all, core * gx * block, block, "x"))
    finish(gather_start(emb_all, 0, gx * block, "core"))

    finish(query_copies)
    lane = lax.broadcasted_iota(jnp.int32, (meta_rows, 128), 1)
    want_tiles, flag_tiles = [], []
    for t in range(nq // per):
        want = jnp.zeros((1, 128), jnp.int32)
        flag = jnp.zeros((meta_rows, 128), F32)
        for h in range(per):
            sent = meta_in[t * per + h]
            want = want + sent[ni : ni + 1, :]
            column = jnp.sum(jnp.where(lane == q, sent, 0).astype(F32), axis=1, keepdims=True)
            inside = (lane >= h * q_rows) & (lane < (h + 1) * q_rows)
            flag = flag + jnp.where(inside, column, 0.0)
        want_tiles.append(want)
        flag_tiles.append(flag)
    wanted = jnp.concatenate(want_tiles, axis=1)
    flags_all[...] = jnp.concatenate(flag_tiles, axis=1)

    def located(p):
        item = lax.rem(p, gx) * 2 + lax.div(p, gx)
        first = (item * nq + q) * block
        ids = lax.broadcasted_iota(jnp.int32, (block, n_q), 0)
        hit = ids == (wanted - first)
        live = flags_all[pl.ds(item, 1), :] > 0.5
        return hit, live

    def score_block(p, carried):
        top, total, positive = carried
        hit, live = located(p)
        s = 0.25 * dot(emb_all[rows(p * block, block), :], q_all[...], (1, 1))
        scores[rows(p * block, block), :] = s
        here = jnp.max(s, axis=0, keepdims=True)
        added = jnp.sum(jnp.exp(s - here), axis=0, keepdims=True)
        positive = positive + jnp.sum(jnp.where(hit, s, 0.0), axis=0, keepdims=True)
        here = jnp.where(live, here, -1e30)
        new_top = jnp.maximum(top, here)
        total = total * jnp.exp(top - new_top) + jnp.where(live, added * jnp.exp(here - new_top), 0.0)
        return new_top, total, positive

    start = (jnp.full((1, n_q), -1e30, F32), jnp.zeros((1, n_q), F32), jnp.zeros((1, n_q), F32))
    top, total, positive = lax.fori_loop(0, ni, score_block, start)
    stats_all[0] = jnp.concatenate([top, total, positive, jnp.zeros((5, n_q), F32)], axis=0)
    finish([
        send(stats_all.at[0], stats_all.at[k], {"query": lax.rem(q + k, nq)}) for k in range(1, nq)
    ])
    top = stats_all[0, 0:1, :]
    for k in range(1, nq):
        top = jnp.maximum(top, stats_all[k, 0:1, :])
    total = jnp.zeros((1, n_q), F32)
    positive = jnp.zeros((1, n_q), F32)
    for k in range(nq):
        total = total + stats_all[k, 1:2, :] * jnp.exp(stats_all[k, 0:1, :] - top)
        positive = positive + stats_all[k, 2:3, :]
    log_norm = top + jnp.log(total)
    stats_all[0, 0:1, :] = log_norm - positive
    found = stats_all[0, 0:1, pl.ds(pl.multiple_of(lax.div(q_pos, per) * 128, 128), 128)]
    moved = found
    for h in range(1, per):
        moved = jnp.where(lax.rem(q_pos, per) == h, pltpu.roll(found, (per - h) * q_rows, 1), moved)
    loss_ref[...] = moved[:, :q_rows]

    def grad_block(p, carried):
        hit, live = located(p)
        s = scores[rows(p * block, block), :]
        weights = jnp.where(live, jnp.exp(s - log_norm), 0.0)
        c = (weights - hit.astype(F32)).astype(BF16)
        coeffs[rows(p * block, block), :] = c
        e_acc[rows(p * block, block), :] = 0.25 * dot(c, q_all[...], (1, 0))
        return carried

    e_size = gx * block
    pairs = []
    for k in list(range(1, gx)) + [0]:
        t = lax.rem(x + k, gx)
        grad_block((1 - core) * gx + t, 0)
        leaving = rows(((1 - core) * gx + t) * block, block)
        landed = e_recv_c.at[rows(t * block, block)]
        pairs.append(send(e_acc.at[leaving], landed, {"item": x * 2 + 1 - core}))
        grad_block(core * gx + t, 0)
        if k > 0:
            here = rows((core * gx + t) * block, block)
            pairs[-1].wait()
            e_acc[here, :] = e_acc[here, :] + e_recv_c[rows(t * block, block), :]
            pairs[-1] = send(e_acc.at[here], e_recv_x.at[rows((k - 1) * block, block)], {"item": t * 2 + core})
    q_acc[...] = 0.25 * dot(coeffs[...], emb_all[...], (0, 0))
    q_copies = reduce_start(q_acc, q_recv_y, 0, gz * q_rows, "y")
    e_base = (core * gx + x) * block
    pairs[-1].wait()
    e_acc[rows(e_base, block), :] = e_acc[rows(e_base, block), :] + e_recv_c[rows(x * block, block), :]
    e_base = reduce_finish(pairs[:-1], e_acc, e_recv_x, core * gx * block, block, "x")
    own_grad = e_acc[rows(e_base, block), :].astype(BF16)

    hid, din = w2_ref.shape[0], tokens.shape[1]
    part = b_acc.shape[0]
    chains = [
        {"acc": a_acc, "out": a_out, "first": 0, "order": ("core", "x", "y", "zl", "zh")},
        {"acc": a_acc, "out": a_out, "first": part, "order": ("core", "y", "x", "zl", "zh")},
        {"acc": b_acc, "out": b_out, "first": 0, "order": ("core", "zl", "zh", "x", "y")},
    ]
    landing = {"core": core_recv, "x": x_recv, "y": y_recv, "zl": l_recv, "zh": h_recv}

    def descend(n):
        chain = chains[n]
        level = chain.setdefault("level", 0)
        if level == 0:
            chain["base"], chain["size"] = chain["first"], part
        else:
            chain["base"] = reduce_finish(
                chain["copies"], chain["acc"], landing[chain["order"][level - 1]].at[n],
                chain["base"], chain["size"], chain["order"][level - 1],
            )
        if level < 5:
            axis = chain["order"][level]
            chain["size"] = chain["size"] // axes[axis][0]
            chain["copies"] = reduce_start(
                chain["acc"], landing[axis].at[n], chain["base"], chain["size"], axis
            )
            chain["level"] = level + 1
        else:
            here = rows(chain["base"], chain["size"])
            chain["out"][here, :] = (chain["acc"][here, :] * grad_scale).astype(chain["out"].dtype)
            chain["copies"] = []

    def ascend(n):
        chain = chains[n]
        finish(chain["copies"])
        level = chain["level"] - 1
        chain["level"] = level
        if level < 0:
            return
        group, own, _ = axes[chain["order"][level]]
        chain["base"] = chain["base"] - own * chain["size"]
        chain["copies"] = gather_start(
            chain["out"], chain["base"], chain["size"], chain["order"][level]
        )
        chain["size"] = chain["size"] * group

    second = dot(hidden[...], own_grad, (0, 0))
    for j in range(width // 128):
        b_acc[j * hid : (j + 1) * hid, :] = second[:, j * 128 : (j + 1) * 128]
    descend(2)
    q_base = reduce_finish(q_copies, q_acc, q_recv_y, 0, gz * q_rows, "y")
    q_copies = reduce_start(q_acc, q_recv_l, q_base, gh * q_rows, "zl")
    hid_grad = dot(own_grad, w2_ref[...], (1, 1))
    pre = pre_act[...]
    sig = jax.nn.sigmoid(pre)
    pre_grad = (hid_grad * sig * (1.0 + pre * (1.0 - sig))).astype(BF16)
    half = hid // 2
    for n in range(2):
        first = dot(tokens, pre_grad[:, n * half : (n + 1) * half], (0, 0))
        for j in range(half // 128):
            start_row = n * part + j * din
            a_acc[start_row : start_row + din, :] = first[:, j * 128 : (j + 1) * 128]
        descend(n)
        if n == 0:
            descend(2)
            q_base = reduce_finish(q_copies, q_acc, q_recv_l, q_base, gh * q_rows, "zl")
            q_copies = reduce_start(q_acc, q_recv_h, q_base, q_rows, "zh")
    for n in (0, 1, 2, 0, 1):
        descend(n)
    q_base = reduce_finish(q_copies, q_acc, q_recv_h, q_base, q_rows, "zh")
    qgrad_ref[...] = q_acc[rows(q_base, q_rows), :]
    for n in (2, 0, 1, 2, 0, 1, 2):
        descend(n)
    ascend(2)
    for n in (0, 1):
        descend(n)
        ascend(n)
    for n in (2, 0, 1, 2, 0, 1, 2, 0, 1, 2, 0, 1, 2, 0, 1):
        ascend(n)


def on_device(query_emb, targets, eligible_tiles, item_feats, w_first, w_second):
    q_rows, width = query_emb.shape
    ni, nq = lax.axis_size("item"), lax.axis_size("query")
    gx, gz = ni // 2, nq // 2
    tokens = item_feats.reshape(item_feats.shape[1], item_feats.shape[2])
    block, din = tokens.shape
    hid = w_first.shape[1]
    n_q = nq * q_rows
    meta_rows = -(-(ni + 1) // 8) * 8
    a_rows, b_rows = din * hid // 128, hid * width // 128
    part = b_rows
    out_dtype = BF16 if part // (nq * ni) % 16 == 0 else F32
    n_copies = 3 * (nq - 1) + (ni - 1) + 2 * gx + gx + gz + 3 * 2 * (3 + gx - 1 + gz // 2 - 1)
    vmem = pltpu.VMEM
    loss, query_grad, g1, g2 = pl.pallas_call(
        functools.partial(window_kernel, (nq, ni, 1.0 / math.sqrt(block * nq * ni))),
        out_shape=(
            jax.ShapeDtypeStruct((1, q_rows), F32),
            jax.ShapeDtypeStruct((q_rows, width), F32),
            jax.ShapeDtypeStruct((a_rows, 128), out_dtype),
            jax.ShapeDtypeStruct((b_rows, 128), out_dtype),
        ),
        in_specs=[pl.BlockSpec(memory_space=vmem)] * 3 + [pl.BlockSpec(memory_space=pl.ANY)] * 3,
        out_specs=(pl.BlockSpec(memory_space=vmem),) * 4,
        scratch_shapes=[
            vmem((block, din), BF16),
            vmem((din, hid), BF16),
            vmem((hid, width), BF16),
            vmem((n_q, width), BF16),
            vmem((ni, meta_rows, 128), jnp.int32),
            vmem((nq, meta_rows, 128), jnp.int32),
            vmem((ni * block, width), BF16),
            vmem((meta_rows, n_q), F32),
            vmem((ni * block, n_q), F32),
            vmem((ni * block, n_q), BF16),
            vmem((nq, 8, n_q), F32),
            vmem((ni * block, width), F32),
            vmem((gx * block, width), F32),
            vmem((max(gx - 1, 1) * block, width), F32),
            vmem((n_q, width), F32),
            vmem((gz * q_rows, width), F32),
            vmem((gz // 2 * q_rows, width), F32),
            vmem((max(gz // 2 - 1, 1) * q_rows, width), F32),
            vmem((block, hid), F32),
            vmem((block, hid), BF16),
            vmem((a_rows, 128), F32),
            vmem((b_rows, 128), F32),
            vmem((3, part // 2, 128), F32),
            vmem((3, part // 2, 128), F32),
            vmem((3, part // 4, 128), F32),
            vmem((3, part // 4, 128), F32),
            vmem((3, part // 4, 128), F32),
            pltpu.SemaphoreType.DMA((n_copies,)),
            pltpu.SemaphoreType.DMA((n_copies,)),
            pltpu.SemaphoreType.DMA((3,)),
        ],
        compiler_params=pltpu.CompilerParams(
            collective_id=0, has_side_effects=True, vmem_limit_bytes=58 * 2**20
        ),
        name="loss_window",
    )(query_emb, targets.reshape(1, -1), eligible_tiles, tokens, w_first, w_second)
    loss = loss.reshape(q_rows)
    g1 = g1.reshape(hid // 128, din, 128).transpose(1, 0, 2).reshape(din, hid).astype(F32)
    g2 = g2.reshape(width // 128, hid, 128).transpose(1, 0, 2).reshape(hid, width).astype(F32)
    return (loss, query_grad, g1, g2)


def solution(mesh):
    return jax.shard_map(
        on_device,
        mesh=mesh,
        in_specs=(
            P(("query", "item"), None),
            P("query"),
            P("query", "item"),
            P("item", "query", None),
            P(),
            P(),
        ),
        out_specs=(P(("query", "item")), P(("query", "item"), None), P(), P()),
        check_vma=False,
    )
```

```python
import functools
import math

import jax
import jax.numpy as jnp
from jax import lax
from jax.experimental import pallas as pl
from jax.experimental.pallas import tpu as pltpu
from jax.sharding import PartitionSpec as P

F32 = jnp.float32
BF16 = jnp.bfloat16


def dot(a, b, contract):
    return lax.dot_general(a, b, ((contract[:1], contract[1:]), ((), ())), preferred_element_type=F32)


def rows(start, size):
    return pl.ds(pl.multiple_of(start, math.gcd(size, 256)), size)


def window_kernel(
    shape,
    query_ref, targets_ref, flags_ref, tokens_hbm, w1_hbm, w2_hbm,
    loss_ref, qgrad_ref, a_out, b_out,
    tokens_ref, w1_ref, w2_ref, q_all, raw_in, meta_in, emb_all, flags_all, scores, coeffs, stats_all,
    e_acc, e_recv_c, e_recv_x, q_acc, q_recv_y, q_recv_l, q_recv_h,
    pre_act, hidden, a_acc, b_acc, core_recv, x_recv, y_recv, l_recv, h_recv,
    send_sems, recv_sems, load_sems,
):
    nq, ni, grad_scale = shape
    gx, gz = ni // 2, nq // 2
    q, i = lax.axis_index("query"), lax.axis_index("item")
    core, x = lax.rem(i, 2), lax.div(i, 2)
    y, z = lax.rem(q, 2), lax.div(q, 2)
    zl, zh = lax.rem(z, 2), lax.div(z, 2)
    gh = gz // 2
    q_rows, width = query_ref.shape
    n_q = nq * q_rows
    block = tokens_ref.shape[0]
    used = [0]
    loads = [
        pltpu.make_async_copy(src, dst, load_sems.at[n])
        for n, (src, dst) in enumerate(((tokens_hbm, tokens_ref), (w1_hbm, w1_ref), (w2_hbm, w2_ref)))
    ]
    for load in loads:
        load.start()

    def send(src, dst, peer):
        slot = used[0]
        used[0] += 1
        copy = pltpu.make_async_remote_copy(
            src_ref=src, dst_ref=dst, send_sem=send_sems.at[slot], recv_sem=recv_sems.at[slot],
            device_id=peer, device_id_type=pl.DeviceIdType.MESH,
        )
        copy.start()
        return copy

    def finish(copies):
        for copy in copies:
            copy.wait()

    axes = {
        "core": (2, core, lambda t: {"item": x * 2 + t}),
        "x": (gx, x, lambda t: {"item": t * 2 + core}),
        "y": (2, y, lambda t: {"query": z * 2 + t}),
        "z": (gz, z, lambda t: {"query": t * 2 + y}),
        "zl": (2, zl, lambda t: {"query": (zh * 2 + t) * 2 + y}),
        "zh": (gh, zh, lambda t: {"query": (t * 2 + zl) * 2 + y}),
    }

    def reduce_start(acc, recv, base, size, axis):
        group, own, peer = axes[axis]
        copies = []
        for k in range(1, group):
            there = lax.rem(own + k, group)
            copies.append(
                send(acc.at[rows(base + there * size, size)], recv.at[rows((k - 1) * size, size)], peer(there))
            )
        return copies

    def reduce_finish(copies, acc, recv, base, size, axis):
        group, own, _ = axes[axis]
        finish(copies)
        here = rows(base + own * size, size)
        total = acc[here, :]
        for k in range(1, group):
            total = total + recv[rows((k - 1) * size, size), :]
        acc[here, :] = total
        return base + own * size

    def gather_start(buf, base, size, axis):
        group, own, peer = axes[axis]
        here = buf.at[rows(base + own * size, size)]
        return [send(here, here, peer(lax.rem(own + k, group))) for k in range(1, group)]

    barrier = pltpu.get_barrier_semaphore()
    for k in range(1, nq):
        pl.semaphore_signal(
            barrier, inc=1, device_id={"query": lax.rem(q + k, nq)}, device_id_type=pl.DeviceIdType.MESH
        )
    for k in range(1, ni):
        pl.semaphore_signal(
            barrier, inc=1, device_id={"item": lax.rem(i + k, ni)}, device_id_type=pl.DeviceIdType.MESH
        )
    pl.semaphore_wait(barrier, nq + ni - 2)

    q_pos = (y * 2 + zl) * gh + zh
    query_copies = []
    for k in range(1, nq):
        there = lax.rem(q + k, nq)
        query_copies.append(send(query_ref, q_all.at[rows(q_pos * q_rows, q_rows)], {"query": there}))
    per = 128 // q_rows
    meta_rows = raw_in.shape[1]
    raw_in[i] = jnp.zeros((meta_rows, 128), jnp.int32)
    raw_in[i, 0:ni, 0:nq] = (flags_ref[...] > 0).astype(jnp.int32)
    raw_copies = [send(raw_in.at[i], raw_in.at[i], {"item": lax.rem(i + k, ni)}) for k in range(1, ni)]
    q_all[rows(q_pos * q_rows, q_rows), :] = query_ref[...]
    lane_row = lax.broadcasted_iota(jnp.int32, (1, 128), 1)
    first_lane = pl.multiple_of(lax.div(i, per) * 128, 128)
    found = targets_ref[:, pl.ds(first_lane, 128)]
    shift = lax.rem(q_pos - i + per * nq * ni, per)
    moved = found
    for h in range(1, per):
        moved = jnp.where(shift == h, pltpu.roll(found, h * q_rows, 1), moved)
    inside = lax.div(lane_row, q_rows) == lax.rem(q_pos, per)
    own_targets = jnp.where(inside, moved, 0)
    loads[0].wait()
    loads[1].wait()
    tokens = tokens_ref[...]
    pre = dot(tokens, w1_ref[...], (1, 0))
    pre_act[...] = pre
    finish(raw_copies)
    parts = [raw_in[t, pl.ds(i, 1), :] for t in range(ni)] + [own_targets]
    if meta_rows > ni + 1:
        parts.append(jnp.zeros((meta_rows - ni - 1, 128), jnp.int32))
    meta_in[q_pos] = jnp.concatenate(parts, axis=0)
    for k in range(1, nq):
        query_copies.append(send(meta_in.at[q_pos], meta_in.at[q_pos], {"query": lax.rem(q + k, nq)}))
    loads[2].wait()
    hidden[...] = jax.nn.silu(pre).astype(BF16)
    i_pos = core * gx + x
    emb_all[rows(i_pos * block, block), :] = dot(hidden[...], w2_ref[...], (1, 0)).astype(BF16)

    finish(gather_start(emb_all, core * gx * block, block, "x"))
    finish(gather_start(emb_all, 0, gx * block, "core"))

    finish(query_copies)
    lane = lax.broadcasted_iota(jnp.int32, (meta_rows, 128), 1)
    want_tiles, flag_tiles = [], []
    for t in range(nq // per):
        want = jnp.zeros((1, 128), jnp.int32)
        flag = jnp.zeros((meta_rows, 128), F32)
        for h in range(per):
            sent = meta_in[t * per + h]
            want = want + sent[ni : ni + 1, :]
            column = jnp.sum(jnp.where(lane == q, sent, 0).astype(F32), axis=1, keepdims=True)
            inside = (lane >= h * q_rows) & (lane < (h + 1) * q_rows)
            flag = flag + jnp.where(inside, column, 0.0)
        want_tiles.append(want)
        flag_tiles.append(flag)
    wanted = jnp.concatenate(want_tiles, axis=1)
    flags_all[...] = jnp.concatenate(flag_tiles, axis=1)

    def located(p):
        item = lax.rem(p, gx) * 2 + lax.div(p, gx)
        first = (item * nq + q) * block
        ids = lax.broadcasted_iota(jnp.int32, (block, n_q), 0)
        hit = ids == (wanted - first)
        live = flags_all[pl.ds(item, 1), :] > 0.5
        return hit, live

    def score_block(p, carried):
        top, total, positive = carried
        hit, live = located(p)
        s = 0.25 * dot(emb_all[rows(p * block, block), :], q_all[...], (1, 1))
        scores[rows(p * block, block), :] = s
        here = jnp.max(s, axis=0, keepdims=True)
        added = jnp.sum(jnp.exp(s - here), axis=0, keepdims=True)
        positive = positive + jnp.sum(jnp.where(hit, s, 0.0), axis=0, keepdims=True)
        here = jnp.where(live, here, -1e30)
        new_top = jnp.maximum(top, here)
        total = total * jnp.exp(top - new_top) + jnp.where(live, added * jnp.exp(here - new_top), 0.0)
        return new_top, total, positive

    start = (jnp.full((1, n_q), -1e30, F32), jnp.zeros((1, n_q), F32), jnp.zeros((1, n_q), F32))
    top, total, positive = lax.fori_loop(0, ni, score_block, start)
    stats_all[0] = jnp.concatenate([top, total, positive, jnp.zeros((5, n_q), F32)], axis=0)
    finish([
        send(stats_all.at[0], stats_all.at[k], {"query": lax.rem(q + k, nq)}) for k in range(1, nq)
    ])
    top = stats_all[0, 0:1, :]
    for k in range(1, nq):
        top = jnp.maximum(top, stats_all[k, 0:1, :])
    total = jnp.zeros((1, n_q), F32)
    positive = jnp.zeros((1, n_q), F32)
    for k in range(nq):
        total = total + stats_all[k, 1:2, :] * jnp.exp(stats_all[k, 0:1, :] - top)
        positive = positive + stats_all[k, 2:3, :]
    log_norm = top + jnp.log(total)
    stats_all[0, 0:1, :] = log_norm - positive
    found = stats_all[0, 0:1, pl.ds(pl.multiple_of(lax.div(q_pos, per) * 128, 128), 128)]
    moved = found
    for h in range(1, per):
        moved = jnp.where(lax.rem(q_pos, per) == h, pltpu.roll(found, (per - h) * q_rows, 1), moved)
    loss_ref[...] = moved[:, :q_rows]

    def grad_block(p, carried):
        hit, live = located(p)
        s = scores[rows(p * block, block), :]
        weights = jnp.where(live, jnp.exp(s - log_norm), 0.0)
        c = (weights - hit.astype(F32)).astype(BF16)
        coeffs[rows(p * block, block), :] = c
        e_acc[rows(p * block, block), :] = 0.25 * dot(c, q_all[...], (1, 0))
        return carried

    e_size = gx * block
    pairs = []
    for k in list(range(1, gx)) + [0]:
        t = lax.rem(x + k, gx)
        grad_block((1 - core) * gx + t, 0)
        leaving = rows(((1 - core) * gx + t) * block, block)
        landed = e_recv_c.at[rows(t * block, block)]
        pairs.append(send(e_acc.at[leaving], landed, {"item": x * 2 + 1 - core}))
        grad_block(core * gx + t, 0)
        if k > 0:
            here = rows((core * gx + t) * block, block)
            pairs[-1].wait()
            e_acc[here, :] = e_acc[here, :] + e_recv_c[rows(t * block, block), :]
            pairs[-1] = send(e_acc.at[here], e_recv_x.at[rows((k - 1) * block, block)], {"item": t * 2 + core})
    q_acc[...] = 0.25 * dot(coeffs[...], emb_all[...], (0, 0))
    q_copies = reduce_start(q_acc, q_recv_y, 0, gz * q_rows, "y")
    e_base = (core * gx + x) * block
    pairs[-1].wait()
    e_acc[rows(e_base, block), :] = e_acc[rows(e_base, block), :] + e_recv_c[rows(x * block, block), :]
    e_base = reduce_finish(pairs[:-1], e_acc, e_recv_x, core * gx * block, block, "x")
    own_grad = e_acc[rows(e_base, block), :].astype(BF16)

    hid, din = w2_ref.shape[0], tokens.shape[1]
    part = b_acc.shape[0]
    chains = [
        {"acc": a_acc, "out": a_out, "first": 0, "order": ("core", "x", "y", "z")},
        {"acc": a_acc, "out": a_out, "first": part, "order": ("core", "y", "x", "z")},
        {"acc": b_acc, "out": b_out, "first": 0, "order": ("core", "zl", "zh", "x", "y")},
    ]
    landing = {"core": core_recv, "x": x_recv, "y": y_recv, "zl": l_recv, "zh": h_recv, "z": h_recv}

    def descend(n):
        chain = chains[n]
        level = chain.setdefault("level", 0)
        if level == 0:
            chain["base"], chain["size"] = chain["first"], part
        else:
            chain["base"] = reduce_finish(
                chain["copies"], chain["acc"], landing[chain["order"][level - 1]].at[n],
                chain["base"], chain["size"], chain["order"][level - 1],
            )
        if level < len(chain["order"]):
            axis = chain["order"][level]
            chain["size"] = chain["size"] // axes[axis][0]
            chain["copies"] = reduce_start(
                chain["acc"], landing[axis].at[n], chain["base"], chain["size"], axis
            )
            chain["level"] = level + 1
        else:
            here = rows(chain["base"], chain["size"])
            chain["out"][here, :] = (chain["acc"][here, :] * grad_scale).astype(chain["out"].dtype)
            chain["copies"] = []

    def ascend(n):
        chain = chains[n]
        finish(chain["copies"])
        level = chain["level"] - 1
        chain["level"] = level
        if level < 0:
            return
        group, own, _ = axes[chain["order"][level]]
        chain["base"] = chain["base"] - own * chain["size"]
        chain["copies"] = gather_start(
            chain["out"], chain["base"], chain["size"], chain["order"][level]
        )
        chain["size"] = chain["size"] * group

    second = dot(hidden[...], own_grad, (0, 0))
    for j in range(width // 128):
        b_acc[j * hid : (j + 1) * hid, :] = second[:, j * 128 : (j + 1) * 128]
    descend(2)
    q_base = reduce_finish(q_copies, q_acc, q_recv_y, 0, gz * q_rows, "y")
    q_copies = reduce_start(q_acc, q_recv_l, q_base, gh * q_rows, "zl")
    hid_grad = dot(own_grad, w2_ref[...], (1, 1))
    pre = pre_act[...]
    sig = jax.nn.sigmoid(pre)
    pre_grad = (hid_grad * sig * (1.0 + pre * (1.0 - sig))).astype(BF16)
    half = hid // 2
    for n in range(2):
        first = dot(tokens, pre_grad[:, n * half : (n + 1) * half], (0, 0))
        for j in range(half // 128):
            start_row = n * part + j * din
            a_acc[start_row : start_row + din, :] = first[:, j * 128 : (j + 1) * 128]
        descend(n)
        if n == 0:
            descend(2)
            q_base = reduce_finish(q_copies, q_acc, q_recv_l, q_base, gh * q_rows, "zl")
            q_copies = reduce_start(q_acc, q_recv_h, q_base, q_rows, "zh")
    for n in (0, 1, 2, 0, 1):
        descend(n)
    q_base = reduce_finish(q_copies, q_acc, q_recv_h, q_base, q_rows, "zh")
    qgrad_ref[...] = q_acc[rows(q_base, q_rows), :]
    for n in (0, 1, 2, 2, 2):
        descend(n)
    ascend(2)
    for n in (0, 1):
        descend(n)
        ascend(n)
    for n in (2, 0, 1, 2, 0, 1, 2, 0, 1, 2, 0, 1, 2):
        ascend(n)


def on_device(query_emb, targets, eligible_tiles, item_feats, w_first, w_second):
    q_rows, width = query_emb.shape
    ni, nq = lax.axis_size("item"), lax.axis_size("query")
    gx, gz = ni // 2, nq // 2
    tokens = item_feats.reshape(item_feats.shape[1], item_feats.shape[2])
    block, din = tokens.shape
    hid = w_first.shape[1]
    n_q = nq * q_rows
    meta_rows = -(-(ni + 1) // 8) * 8
    a_rows, b_rows = din * hid // 128, hid * width // 128
    part = b_rows
    out_dtype = BF16 if part // (nq * ni) % 16 == 0 else F32
    n_copies = 3 * (nq - 1) + (ni - 1) + 2 * gx + gx + gz + 3 * 2 * (3 + gx - 1 + gz - 1)
    vmem = pltpu.VMEM
    loss, query_grad, g1, g2 = pl.pallas_call(
        functools.partial(window_kernel, (nq, ni, 1.0 / math.sqrt(block * nq * ni))),
        out_shape=(
            jax.ShapeDtypeStruct((1, q_rows), F32),
            jax.ShapeDtypeStruct((q_rows, width), F32),
            jax.ShapeDtypeStruct((a_rows, 128), out_dtype),
            jax.ShapeDtypeStruct((b_rows, 128), out_dtype),
        ),
        in_specs=[pl.BlockSpec(memory_space=vmem)] * 3 + [pl.BlockSpec(memory_space=pl.ANY)] * 3,
        out_specs=(pl.BlockSpec(memory_space=vmem),) * 4,
        scratch_shapes=[
            vmem((block, din), BF16),
            vmem((din, hid), BF16),
            vmem((hid, width), BF16),
            vmem((n_q, width), BF16),
            vmem((ni, meta_rows, 128), jnp.int32),
            vmem((nq, meta_rows, 128), jnp.int32),
            vmem((ni * block, width), BF16),
            vmem((meta_rows, n_q), F32),
            vmem((ni * block, n_q), F32),
            vmem((ni * block, n_q), BF16),
            vmem((nq, 8, n_q), F32),
            vmem((ni * block, width), F32),
            vmem((gx * block, width), F32),
            vmem((max(gx - 1, 1) * block, width), F32),
            vmem((n_q, width), F32),
            vmem((gz * q_rows, width), F32),
            vmem((gz // 2 * q_rows, width), F32),
            vmem((max(gz // 2 - 1, 1) * q_rows, width), F32),
            vmem((block, hid), F32),
            vmem((block, hid), BF16),
            vmem((a_rows, 128), F32),
            vmem((b_rows, 128), F32),
            vmem((3, part // 2, 128), F32),
            vmem((3, part // 2, 128), F32),
            vmem((3, part // 4, 128), F32),
            vmem((3, part // 4, 128), F32),
            vmem((3, part // 4, 128), F32),
            pltpu.SemaphoreType.DMA((n_copies,)),
            pltpu.SemaphoreType.DMA((n_copies,)),
            pltpu.SemaphoreType.DMA((3,)),
        ],
        compiler_params=pltpu.CompilerParams(
            collective_id=0, has_side_effects=True, vmem_limit_bytes=58 * 2**20
        ),
        name="loss_window",
    )(query_emb, targets.reshape(1, -1), eligible_tiles, tokens, w_first, w_second)
    loss = loss.reshape(q_rows)
    g1 = g1.reshape(hid // 128, din, 128).transpose(1, 0, 2).reshape(din, hid).astype(F32)
    g2 = g2.reshape(width // 128, hid, 128).transpose(1, 0, 2).reshape(hid, width).astype(F32)
    return (loss, query_grad, g1, g2)


def solution(mesh):
    return jax.shard_map(
        on_device,
        mesh=mesh,
        in_specs=(
            P(("query", "item"), None),
            P("query"),
            P("query", "item"),
            P("item", "query", None),
            P(),
            P(),
        ),
        out_specs=(P(("query", "item")), P(("query", "item"), None), P(), P()),
        check_vma=False,
    )
```
